32 devices in a mesh: expert: 2 (over y), blk: 16 (over z, x, core).
Axes of the slice: x: 2, y: 2, z: 4, core: 2. Of those that a mesh axis runs over, the one named last changes fastest.
Arguments:
- query_grads: bfloat16 [2, 16384, 2304], P('expert', 'blk'), may hold values from -0.125 to 0.125
- train_grads: bfloat16 [2, 128, 2304], P('expert', 'blk'), may hold values from -6 to 6
- counts: int32 [2, 128], P('expert', 'blk'), may hold values from 0 to 64
- factor: bfloat16 [2, 2304, 2304], P('expert', 'blk'), as said below
Outputs:
- scores: float32 [16384, 128], P('blk', 'expert')
The draws below stay inside these ranges and needn't reach their ends.
Inputs may be any that keep to these rules, and one draw needn't show every extreme that they name: counts of tokens of one example, 0 where the expert gets none of them. Each expert's factor has the largest entry of each row on its diagonal.
All inputs are finite; a program needn't handle non-finite values.
Results may differ from the reference program's by a relative error of at most 0.0038.
Values may be sent and summed in bfloat16 or wider, within the bound.
A program may use at most 64 MiB of HBM per device.

```python
import math
import jax
import jax.numpy as jnp
from jax import lax

K = 2304
TOKS_EX = 64
EXPERTS = 2
Q_ALL = 16384
T_ALL = 128


def draw_factor(key, part):
    base = jax.random.fold_in(key, 7)
    noise_key, scale_key = jax.random.split(base, 2)
    noise = jax.random.normal(noise_key, (EXPERTS, K, K), jnp.float32) * (0.5 / math.sqrt(K))
    row_scales = jnp.exp(jax.random.uniform(scale_key, (EXPERTS, K, 1), jnp.float32, math.log(0.4), math.log(2.5)))
    identity = jnp.eye(K, dtype=jnp.float32)[None, :, :]
    return (row_scales * (identity + noise)).astype(jnp.bfloat16)


def place_ends(array, stream_key, low, high):
    dims = array.shape
    index_at = [jax.random.randint(jax.random.fold_in(stream_key, axis), (), 0, dims[axis]) for axis in range(len(dims))]
    array = array.at[tuple(index_at)].set(low)
    longest = dims.index(max(dims))
    index_at[longest] = (index_at[longest] + 1) % dims[longest]
    return array.at[tuple(index_at)].set(high)


def steps_of(stream_key, extent, cuts, low, largest):
    level, own = 1.0, jax.random.fold_in(stream_key, 6)
    for axis_at, shards_of in cuts:
        heights = jnp.exp(jax.random.uniform(jax.random.fold_in(own, axis_at), (shards_of,), jnp.float32, low / len(cuts), largest / len(cuts)))
        level = level * jnp.repeat(heights, extent[axis_at] // shards_of).reshape([-1 if axis == axis_at else 1 for axis in range(len(extent))])
    return level


def bell_draw(own_key, extent, deviation, most, shards=(), held_as=jnp.bfloat16):
    level = steps_of(own_key, extent, shards, -0.22, 0.18) if shards else 1.0
    array = jax.random.normal(own_key, extent, jnp.float32) * deviation * level
    return jnp.minimum(jnp.maximum(array, -most), most).astype(held_as)


def setup_inputs(seed: int = 0) -> dict:
    arg_keys = jax.random.split(jax.random.key(seed), 5)
    return {
        "query_grads": bell_draw(arg_keys[0], (EXPERTS, Q_ALL, K), K ** -0.5, 0.125, ((0, 2), (1, 16))),
        "train_grads": bell_draw(arg_keys[1], (EXPERTS, T_ALL, K), 1.0, 6.0, ((0, 2), (1, 16))),
        "counts": place_ends(jax.random.randint(arg_keys[2], (EXPERTS, T_ALL), 0, TOKS_EX + 1), jax.random.fold_in(arg_keys[2], 1), 0, TOKS_EX).astype(jnp.int32),
        "factor": draw_factor(jax.random.fold_in(arg_keys[4], 71), 0),
    }


def reference(query_grads, train_grads, counts, factor):
    def add_expert(totals, inputs):
        query_rows, train_rows, count_row, factor_block = inputs
        pre_train = jnp.dot(train_rows, factor_block, preferred_element_type=jnp.float32).astype(jnp.bfloat16)
        kernel = jnp.dot(pre_train, factor_block.T, preferred_element_type=jnp.float32).astype(jnp.bfloat16)
        products = jnp.dot(query_rows, kernel.T, preferred_element_type=jnp.float32)
        weights = count_row.astype(jnp.float32) / TOKS_EX
        return totals + products * weights[None, :], None

    initial = jnp.zeros((Q_ALL, T_ALL), jnp.float32)
    scores, unused = lax.scan(add_expert, initial, (query_grads, train_grads, counts, factor))
    return scores
```

```python
import functools

import jax
import jax.numpy as jnp
import numpy as np
from jax import lax
from jax.experimental import pallas as pl
from jax.experimental.pallas import tpu as pltpu
from jax.sharding import PartitionSpec as P

TOKS_EX = 64
MESH = pl.DeviceIdType.MESH
NT = (((1,), (1,)), ((), ()))
CHUNKS = 4


def kernel(
    n_exp, n_chip,
    counts_ref, train_ref, place_ref, query_hbm, factor_hbm, out_ref,
    query, factor, train_out, train_in, part, part_out, part_in,
    pre_out, pre_in, ker, kmat, score, score_in,
    query_sem, own_sem, pair_send, pair_recv,
    a_send, a_recv, b_send, b_recv, c_send, c_recv, d_send, d_recv,
    f_send, f_recv, e_send, e_recv,
):
    expert, blk = lax.axis_index("expert"), lax.axis_index("blk")
    chip, core = blk // 2, blk % 2
    mate = chip * 2 + (1 - core)
    peers = [lax.rem(chip + k, n_chip) for k in range(1, n_chip)]
    rivals = [lax.rem(expert + k, n_exp) for k in range(1, n_exp)]
    t_loc, depth = train_ref.shape[0], factor_hbm.shape[0]
    t_plane = t_loc * n_chip
    wide = 2 * depth

    own_copy = pltpu.make_async_copy(factor_hbm, factor.at[core], own_sem)
    own_copy.start()
    query_copy = pltpu.make_async_copy(query_hbm, query, query_sem)
    query_copy.start()

    barrier = pltpu.get_barrier_semaphore()
    for peer in peers:
        pl.semaphore_signal(barrier, inc=1, device_id=(expert, peer * 2 + core), device_id_type=MESH)
    pl.semaphore_signal(barrier, inc=1, device_id=(expert, mate), device_id_type=MESH)
    for rival in rivals:
        pl.semaphore_signal(barrier, inc=1, device_id=(rival, blk), device_id_type=MESH)

    train = train_ref[...].astype(jnp.float32)
    for c in range(n_chip):
        train_out[c] = train[:, c * wide:(c + 1) * wide].astype(jnp.bfloat16)
    pl.semaphore_wait(barrier, n_chip - 1 + 1 + n_exp - 1)

    def to_peers(source, target, send, recv):
        copies = []
        for k, peer in enumerate(peers):
            copy = pltpu.make_async_remote_copy(
                src_ref=source(peer), dst_ref=target(chip), send_sem=send.at[k],
                recv_sem=recv.at[chip], device_id=(expert, peer * 2 + core), device_id_type=MESH,
            )
            copy.start()
            copies.append(copy)
        return copies

    def from_peer(source, target, send, recv, k):
        peer = peers[k]
        pltpu.make_async_remote_copy(
            src_ref=source(peer), dst_ref=target(peer), send_sem=send.at[k],
            recv_sem=recv.at[peer], device_id=(expert, peer * 2 + core), device_id_type=MESH,
        ).wait_recv()

    a_args = (lambda c: train_out.at[c], lambda c: train_in.at[c], a_send, a_recv)
    a_copies = to_peers(*a_args)
    pair_copy = pltpu.make_async_remote_copy(
        src_ref=factor_hbm, dst_ref=factor.at[core], send_sem=pair_send, recv_sem=pair_recv,
        device_id=(expert, mate), device_id_type=MESH,
    )
    pair_copy.start()
    train_in[chip] = train_out[chip]
    own_copy.wait()
    pair_copy.wait_recv()
    for k in range(n_chip - 1):
        from_peer(*a_args, k)

    rows = train_in[...].astype(jnp.float32).reshape(t_plane, wide)
    first = rows[:, :depth].astype(jnp.bfloat16)
    second = rows[:, depth:].astype(jnp.bfloat16)
    share = jnp.dot(first, factor[0], preferred_element_type=jnp.float32)
    share = share + jnp.dot(second, factor[1], preferred_element_type=jnp.float32)
    share = share.reshape(n_chip, t_loc, share.shape[-1])
    part[...] = share
    part_out[...] = share.astype(jnp.bfloat16)
    b_args = (lambda c: part_out.at[c], lambda c: part_in.at[c], b_send, b_recv)
    b_copies = to_peers(*b_args)
    total = part[chip]
    for k in range(n_chip - 1):
        from_peer(*b_args, k)
        total = total + part_in[peers[k]].astype(jnp.float32)
    at_row = lax.broadcasted_iota(jnp.int32, total.shape, 0)
    weight = jnp.zeros(total.shape, jnp.float32)
    for i in range(t_loc):
        weight = jnp.where(at_row == i, counts_ref[0, i].astype(jnp.float32) / TOKS_EX, weight)
    pre_out[...] = (total * weight).astype(jnp.bfloat16)

    c_args = (lambda c: pre_out, lambda c: pre_in.at[c], c_send, c_recv)
    c_copies = to_peers(*c_args)
    pre_in[chip] = pre_out[...]
    for k in range(n_chip - 1):
        from_peer(*c_args, k)
    pre = pre_in[...].astype(jnp.float32).reshape(t_plane, pre_in.shape[-1]).astype(jnp.bfloat16)
    halves = [
        lax.dot_general(factor[c], pre, NT, preferred_element_type=jnp.float32) for c in range(2)
    ]
    ker[core, chip] = jnp.concatenate(halves, axis=1).astype(jnp.bfloat16)

    d_args = (lambda c: ker.at[core, chip], lambda c: ker.at[core, c], d_send, d_recv)
    d_copies = to_peers(*d_args)
    f_copies = []

    def pass_on(c, k):
        copy = pltpu.make_async_remote_copy(
            src_ref=ker.at[core, c], dst_ref=ker.at[core, c], send_sem=f_send.at[k],
            recv_sem=f_recv.at[c], device_id=(expert, mate), device_id_type=MESH,
        )
        copy.start()
        f_copies.append(copy)

    pass_on(chip, n_chip - 1)
    for k in range(n_chip - 1):
        from_peer(*d_args, k)
        pass_on(peers[k], k)
    for c in range(n_chip):
        pltpu.make_async_remote_copy(
            src_ref=ker.at[1 - core, c], dst_ref=ker.at[1 - core, c], send_sem=f_send.at[c],
            recv_sem=f_recv.at[c], device_id=(expert, mate), device_id_type=MESH,
        ).wait_recv()

    t_all = 2 * t_plane
    for c in range(n_chip):
        both = jnp.concatenate([ker[0, c], ker[1, c]], axis=1)
        placed = jnp.dot(both, place_ref[...], preferred_element_type=jnp.float32).astype(kmat.dtype)
        for half in range(2):
            start = (2 * c + half) * depth
            kmat[start:start + depth, :] = placed[:, half * t_all:(half + 1) * t_all]

    query_copy.wait()
    matrix = kmat[...].astype(jnp.bfloat16)
    side = query.shape[0] // 2
    step = side // CHUNKS
    t_out = t_all // n_exp
    e_copies = []
    for i in range(CHUNKS):
        at = slice(i * step, (i + 1) * step)
        low = jnp.dot(query[at, :], matrix, preferred_element_type=jnp.float32)
        high = jnp.dot(query[side + i * step:side + (i + 1) * step, :], matrix, preferred_element_type=jnp.float32)
        for g in range(n_exp):
            cols = slice(g * t_out, (g + 1) * t_out)
            score[g, i] = jnp.concatenate([low[:, cols], high[:, cols]], axis=1)
        for k, rival in enumerate(rivals):
            copy = pltpu.make_async_remote_copy(
                src_ref=score.at[rival, i], dst_ref=score_in.at[expert, i],
                send_sem=e_send.at[k, i], recv_sem=e_recv.at[expert, i],
                device_id=(rival, blk), device_id_type=MESH,
            )
            copy.start()
            e_copies.append(copy)
    for i in range(CHUNKS):
        total = score[expert, i]
        for k, rival in enumerate(rivals):
            pltpu.make_async_remote_copy(
                src_ref=score.at[rival, i], dst_ref=score_in.at[rival, i],
                send_sem=e_send.at[k, i], recv_sem=e_recv.at[rival, i],
                device_id=(rival, blk), device_id_type=MESH,
            ).wait_recv()
            total = total + score_in[rival, i]
        out_ref[i * step:(i + 1) * step, :] = total
    pair_copy.wait_send()
    for copy in a_copies + b_copies + c_copies + d_copies + f_copies + e_copies:
        copy.wait_send()


def placement(n_chip, t_loc):
    t_plane = n_chip * t_loc
    t_all = 2 * t_plane
    table = np.zeros((2, 2, t_plane, 2, t_all), np.float32)
    for core in range(2):
        for chip in range(n_chip):
            for i in range(t_loc):
                for half in range(2):
                    table[core, half, chip * t_loc + i, half, (2 * chip + core) * t_loc + i] = 1
    return table.reshape(2 * t_all, 2 * t_all)


def on_device(n_exp, n_blk, query_grads, train_grads, counts, factor):
    n_chip = n_blk // 2
    query_grads, train_grads, factor = query_grads[0], train_grads[0], factor[0]
    q_loc, width = query_grads.shape
    t_loc, depth = train_grads.shape[0], factor.shape[0]
    t_plane = t_loc * n_chip
    t_all = 2 * t_plane
    t_out = t_all // n_exp
    bf16, f32 = jnp.bfloat16, jnp.float32
    place = jnp.asarray(placement(n_chip, t_loc), bf16)
    vmem = pl.BlockSpec(memory_space=pltpu.VMEM)
    hbm = pl.BlockSpec(memory_space=pl.ANY)
    dma = pltpu.SemaphoreType.DMA
    side = q_loc // 2
    packed = pl.pallas_call(
        functools.partial(kernel, n_exp, n_chip),
        out_shape=jax.ShapeDtypeStruct((side, 2 * t_out), f32),
        in_specs=[pl.BlockSpec(memory_space=pltpu.SMEM), vmem, vmem, hbm, hbm],
        out_specs=vmem,
        scratch_shapes=[
            pltpu.VMEM((q_loc, width), bf16),
            pltpu.VMEM((2, depth, width), bf16),
            pltpu.VMEM((n_chip, t_loc, 2 * depth), bf16),
            pltpu.VMEM((n_chip, t_loc, 2 * depth), bf16),
            pltpu.VMEM((n_chip, t_loc, width), f32),
            pltpu.VMEM((n_chip, t_loc, width), bf16),
            pltpu.VMEM((n_chip, t_loc, width), bf16),
            pltpu.VMEM((t_loc, width), bf16),
            pltpu.VMEM((n_chip, t_loc, width), bf16),
            pltpu.VMEM((2, n_chip, depth, 2 * t_plane), bf16),
            pltpu.VMEM((width, t_all), bf16 if depth % 16 == 0 else f32),
            pltpu.VMEM((n_exp, CHUNKS, side // CHUNKS, 2 * t_out), f32),
            pltpu.VMEM((n_exp, CHUNKS, side // CHUNKS, 2 * t_out), f32),
            dma, dma, dma, dma,
            dma((n_chip,)), dma((n_chip,)), dma((n_chip,)), dma((n_chip,)),
            dma((n_chip,)), dma((n_chip,)), dma((n_chip,)), dma((n_chip,)),
            dma((n_chip,)), dma((n_chip,)), dma((n_exp, CHUNKS)), dma((n_exp, CHUNKS)),
        ],
        compiler_params=pltpu.CompilerParams(collective_id=0, has_side_effects=True),
        name="influence",
    )(counts, train_grads, place, query_grads, factor)
    return jnp.concatenate([packed[:, :t_out], packed[:, t_out:]], axis=0)


def solution(mesh):
    return jax.shard_map(
        functools.partial(on_device, mesh.shape["expert"], mesh.shape["blk"]),
        mesh=mesh,
        in_specs=(
            P("expert", "blk", None),
            P("expert", "blk", None),
            P("expert", "blk"),
            P("expert", "blk", None),
        ),
        out_specs=P("blk", "expert"),
        check_vma=False,
    )
```

```python
import functools

import jax
import jax.numpy as jnp
from jax import lax
from jax.experimental import pallas as pl
from jax.experimental.pallas import tpu as pltpu
from jax.sharding import PartitionSpec as P

TOKS_EX = 64
MESH = pl.DeviceIdType.MESH
NT = (((1,), (1,)), ((), ()))
CHUNKS = 4


def kernel(
    n_exp, n_chip,
    counts_ref, train_ref, query_hbm, factor_hbm, out_ref,
    query, factor, train_out, train_in, part, part_out, part_in,
    pre_out, pre_in, ker, kmat, score, score_in,
    query_sem, own_sem, pair_send, pair_recv,
    a_send, a_recv, b_send, b_recv, c_send, c_recv, d_send, d_recv,
    f_send, f_recv, e_send, e_recv,
):
    expert, blk = lax.axis_index("expert"), lax.axis_index("blk")
    chip, core = blk // 2, blk % 2
    mate = chip * 2 + (1 - core)
    peers = [lax.rem(chip + k, n_chip) for k in range(1, n_chip)]
    rivals = [lax.rem(expert + k, n_exp) for k in range(1, n_exp)]
    t_loc, depth = train_ref.shape[0], factor_hbm.shape[0]
    t_plane = t_loc * n_chip
    wide = 2 * depth

    own_copy = pltpu.make_async_copy(factor_hbm, factor.at[core], own_sem)
    own_copy.start()
    query_copy = pltpu.make_async_copy(query_hbm, query, query_sem)
    query_copy.start()

    barrier = pltpu.get_barrier_semaphore()
    for peer in peers:
        pl.semaphore_signal(barrier, inc=1, device_id=(expert, peer * 2 + core), device_id_type=MESH)
    pl.semaphore_signal(barrier, inc=1, device_id=(expert, mate), device_id_type=MESH)
    for rival in rivals:
        pl.semaphore_signal(barrier, inc=1, device_id=(rival, blk), device_id_type=MESH)

    train = train_ref[...].astype(jnp.float32)
    for c in range(n_chip):
        train_out[c] = train[:, c * wide:(c + 1) * wide].astype(jnp.bfloat16)
    pl.semaphore_wait(barrier, n_chip - 1 + 1 + n_exp - 1)

    def to_peers(source, target, send, recv):
        copies = []
        for k, peer in enumerate(peers):
            copy = pltpu.make_async_remote_copy(
                src_ref=source(peer), dst_ref=target(chip), send_sem=send.at[k],
                recv_sem=recv.at[chip], device_id=(expert, peer * 2 + core), device_id_type=MESH,
            )
            copy.start()
            copies.append(copy)
        return copies

    def from_peer(source, target, send, recv, k):
        peer = peers[k]
        pltpu.make_async_remote_copy(
            src_ref=source(peer), dst_ref=target(peer), send_sem=send.at[k],
            recv_sem=recv.at[peer], device_id=(expert, peer * 2 + core), device_id_type=MESH,
        ).wait_recv()

    lines = n_chip // 2
    line, side_of = chip // 2, chip % 2
    along = [lax.rem(line + k, lines) * 2 + side_of for k in range(1, lines)]
    pair = line * 2 + (1 - side_of)

    def gather_copy(source, target, send, recv, k, slot, to):
        return pltpu.make_async_remote_copy(
            src_ref=source, dst_ref=target(slot), send_sem=send.at[k], recv_sem=recv.at[slot],
            device_id=(expert, to * 2 + core), device_id_type=MESH,
        )

    def gather(source, target, send, recv, landed):
        copies = []
        for k, to in enumerate(along):
            copies.append(gather_copy(source, target, send, recv, k, chip, to))
        copies.append(gather_copy(source, target, send, recv, lines - 1, chip, pair))
        for copy in copies:
            copy.start()
        landed(chip, 0)
        for k, other in enumerate(along):
            gather_copy(source, target, send, recv, k, other, other).wait_recv()
            copy = gather_copy(target(other), target, send, recv, lines + k, other, pair)
            copy.start()
            copies.append(copy)
            landed(other, 1 + k)
        for k in range(lines):
            other = lax.rem(line + k, lines) * 2 + (1 - side_of)
            gather_copy(source, target, send, recv, k, other, pair).wait_recv()
            landed(other, lines + k)
        return copies

    a_args = (lambda c: train_out.at[c], lambda c: train_in.at[c], a_send, a_recv)
    a_copies = to_peers(*a_args)
    pair_copy = pltpu.make_async_remote_copy(
        src_ref=factor_hbm, dst_ref=factor.at[core], send_sem=pair_send, recv_sem=pair_recv,
        device_id=(expert, mate), device_id_type=MESH,
    )
    pair_copy.start()
    train_in[chip] = train_out[chip]
    own_copy.wait()
    pair_copy.wait_recv()
    for k in range(n_chip - 1):
        from_peer(*a_args, k)

    rows = train_in[...].astype(jnp.float32).reshape(t_plane, wide)
    first = rows[:, :depth].astype(jnp.bfloat16)
    second = rows[:, depth:].astype(jnp.bfloat16)
    share = jnp.dot(first, factor[0], preferred_element_type=jnp.float32)
    share = share + jnp.dot(second, factor[1], preferred_element_type=jnp.float32)
    share = share.reshape(n_chip, t_loc, share.shape[-1])
    part[...] = share
    part_out[...] = share.astype(jnp.bfloat16)
    b_args = (lambda c: part_out.at[c], lambda c: part_in.at[c], b_send, b_recv)
    b_copies = to_peers(*b_args)
    total = part[chip]
    for k in range(n_chip - 1):
        from_peer(*b_args, k)
        total = total + part_in[peers[k]].astype(jnp.float32)
    at_row = lax.broadcasted_iota(jnp.int32, total.shape, 0)
    weight = jnp.zeros(total.shape, jnp.float32)
    for i in range(t_loc):
        weight = jnp.where(at_row == i, counts_ref[0, i].astype(jnp.float32) / TOKS_EX, weight)
    pre_out[...] = (total * weight).astype(jnp.bfloat16)

    c_copies = gather(pre_out, lambda c: pre_in.at[c], c_send, c_recv, lambda c, k: None)
    pre_in[chip] = pre_out[...]
    pre = pre_in[...].astype(jnp.float32).reshape(t_plane, pre_in.shape[-1]).astype(jnp.bfloat16)
    halves = [
        lax.dot_general(factor[c], pre, NT, preferred_element_type=jnp.float32) for c in range(2)
    ]
    ker[core, chip] = jnp.concatenate(halves, axis=1).astype(jnp.bfloat16)

    f_copies = []

    def pass_on(c, k):
        copy = pltpu.make_async_remote_copy(
            src_ref=ker.at[core, c], dst_ref=ker.at[core, c], send_sem=f_send.at[k],
            recv_sem=f_recv.at[c], device_id=(expert, mate), device_id_type=MESH,
        )
        copy.start()
        f_copies.append(copy)

    d_copies = gather(ker.at[core, chip], lambda c: ker.at[core, c], d_send, d_recv, pass_on)
    for c in range(n_chip):
        pltpu.make_async_remote_copy(
            src_ref=ker.at[1 - core, c], dst_ref=ker.at[1 - core, c], send_sem=f_send.at[c],
            recv_sem=f_recv.at[c], device_id=(expert, mate), device_id_type=MESH,
        ).wait_recv()

    t_all = 2 * t_plane
    for c in range(n_chip):
        even, odd = ker[0, c].astype(jnp.float32), ker[1, c].astype(jnp.float32)
        for half in range(2):
            cols = slice(half * t_plane, (half + 1) * t_plane)
            start = (2 * c + half) * depth
            both = jnp.concatenate([even[:, cols], odd[:, cols]], axis=1)
            kmat[start:start + depth, :] = both.astype(kmat.dtype)

    query_copy.wait()
    matrix = kmat[...].astype(jnp.bfloat16)
    step = query.shape[0] // CHUNKS
    t_out = t_all // n_exp
    e_copies = []
    for i in range(CHUNKS):
        found = jnp.dot(query[i * step:(i + 1) * step, :], matrix, preferred_element_type=jnp.float32).T
        for plane in range(2):
            for c in range(n_chip):
                start = plane * t_plane + c * t_loc
                group, row = divmod((2 * c + plane) * t_loc, t_out)
                score[group, i, row:row + t_loc, :] = found[start:start + t_loc, :]
        for k, rival in enumerate(rivals):
            copy = pltpu.make_async_remote_copy(
                src_ref=score.at[rival, i], dst_ref=score_in.at[expert, i],
                send_sem=e_send.at[k, i], recv_sem=e_recv.at[expert, i],
                device_id=(rival, blk), device_id_type=MESH,
            )
            copy.start()
            e_copies.append(copy)
    for i in range(CHUNKS):
        total = score[expert, i]
        for k, rival in enumerate(rivals):
            pltpu.make_async_remote_copy(
                src_ref=score.at[rival, i], dst_ref=score_in.at[rival, i],
                send_sem=e_send.at[k, i], recv_sem=e_recv.at[rival, i],
                device_id=(rival, blk), device_id_type=MESH,
            ).wait_recv()
            total = total + score_in[rival, i]
        out_ref[:, i * step:(i + 1) * step] = total
    pair_copy.wait_send()
    for copy in a_copies + b_copies + c_copies + d_copies + f_copies + e_copies:
        copy.wait_send()


def on_device(n_exp, n_blk, query_grads, train_grads, counts, factor):
    n_chip = n_blk // 2
    query_grads, train_grads, factor = query_grads[0], train_grads[0], factor[0]
    q_loc, width = query_grads.shape
    t_loc, depth = train_grads.shape[0], factor.shape[0]
    t_plane = t_loc * n_chip
    t_all = 2 * t_plane
    t_out = t_all // n_exp
    bf16, f32 = jnp.bfloat16, jnp.float32
    vmem = pl.BlockSpec(memory_space=pltpu.VMEM)
    hbm = pl.BlockSpec(memory_space=pl.ANY)
    dma = pltpu.SemaphoreType.DMA
    transposed = pl.pallas_call(
        functools.partial(kernel, n_exp, n_chip),
        out_shape=jax.ShapeDtypeStruct((t_out, q_loc), f32),
        in_specs=[pl.BlockSpec(memory_space=pltpu.SMEM), vmem, hbm, hbm],
        out_specs=vmem,
        scratch_shapes=[
            pltpu.VMEM((q_loc, width), bf16),
            pltpu.VMEM((2, depth, width), bf16),
            pltpu.VMEM((n_chip, t_loc, 2 * depth), bf16),
            pltpu.VMEM((n_chip, t_loc, 2 * depth), bf16),
            pltpu.VMEM((n_chip, t_loc, width), f32),
            pltpu.VMEM((n_chip, t_loc, width), bf16),
            pltpu.VMEM((n_chip, t_loc, width), bf16),
            pltpu.VMEM((t_loc, width), bf16),
            pltpu.VMEM((n_chip, t_loc, width), bf16),
            pltpu.VMEM((2, n_chip, depth, 2 * t_plane), bf16),
            pltpu.VMEM((width, t_all), bf16 if depth % 16 == 0 else f32),
            pltpu.VMEM((n_exp, CHUNKS, t_out, q_loc // CHUNKS), f32),
            pltpu.VMEM((n_exp, CHUNKS, t_out, q_loc // CHUNKS), f32),
            dma, dma, dma, dma,
            dma((n_chip,)), dma((n_chip,)), dma((n_chip,)), dma((n_chip,)),
            dma((n_chip,)), dma((n_chip,)), dma((n_chip,)), dma((n_chip,)),
            dma((n_chip,)), dma((n_chip,)), dma((n_exp, CHUNKS)), dma((n_exp, CHUNKS)),
        ],
        compiler_params=pltpu.CompilerParams(collective_id=0, has_side_effects=True),
        name="influence",
    )(counts, train_grads, query_grads, factor)
    return transposed.T


def solution(mesh):
    return jax.shard_map(
        functools.partial(on_device, mesh.shape["expert"], mesh.shape["blk"]),
        mesh=mesh,
        in_specs=(
            P("expert", "blk", None),
            P("expert", "blk", None),
            P("expert", "blk"),
            P("expert", "blk", None),
        ),
        out_specs=P("blk", "expert"),
        check_vma=False,
    )
```

```python
import functools

import jax
import jax.numpy as jnp
from jax import lax
from jax.experimental import pallas as pl
from jax.experimental.pallas import tpu as pltpu
from jax.sharding import PartitionSpec as P

TOKS_EX = 64
MESH = pl.DeviceIdType.MESH
NT = (((1,), (1,)), ((), ()))
CHUNKS = 4


def kernel(
    n_exp, n_chip,
    counts_ref, train_ref, query_hbm, factor_hbm, out_ref,
    query, factor, train_out, train_in, part, part_out, part_in, near_in,
    pre_out, pre_in, ker, kmat, score, score_out, score_in,
    query_sem, own_sem, pair_send, pair_recv,
    a_send, a_recv, b_send, b_recv, c_send, c_recv, d_send, d_recv,
    f_send, f_recv, e_send, e_recv,
):
    expert, blk = lax.axis_index("expert"), lax.axis_index("blk")
    chip, core = blk // 2, blk % 2
    mate = chip * 2 + (1 - core)
    peers = [lax.rem(chip + k, n_chip) for k in range(1, n_chip)]
    rivals = [lax.rem(expert + k, n_exp) for k in range(1, n_exp)]
    t_loc, depth = train_ref.shape[0], factor_hbm.shape[0]
    t_plane = t_loc * n_chip
    wide = 2 * depth

    own_copy = pltpu.make_async_copy(factor_hbm, factor.at[core], own_sem)
    own_copy.start()
    query_copy = pltpu.make_async_copy(query_hbm, query, query_sem)
    query_copy.start()

    barrier = pltpu.get_barrier_semaphore()
    for peer in peers:
        pl.semaphore_signal(barrier, inc=1, device_id=(expert, peer * 2 + core), device_id_type=MESH)
    pl.semaphore_signal(barrier, inc=1, device_id=(expert, mate), device_id_type=MESH)
    for rival in rivals:
        pl.semaphore_signal(barrier, inc=1, device_id=(rival, blk), device_id_type=MESH)

    train = train_ref[...].astype(jnp.float32)
    for c in range(n_chip):
        train_out[c] = train[:, c * wide:(c + 1) * wide].astype(jnp.bfloat16)
    pl.semaphore_wait(barrier, n_chip - 1 + 1 + n_exp - 1)

    def to_peers(source, target, send, recv):
        copies = []
        for k, peer in enumerate(peers):
            copy = pltpu.make_async_remote_copy(
                src_ref=source(peer), dst_ref=target(chip), send_sem=send.at[k],
                recv_sem=recv.at[chip], device_id=(expert, peer * 2 + core), device_id_type=MESH,
            )
            copy.start()
            copies.append(copy)
        return copies

    def from_peer(source, target, send, recv, k):
        peer = peers[k]
        pltpu.make_async_remote_copy(
            src_ref=source(peer), dst_ref=target(peer), send_sem=send.at[k],
            recv_sem=recv.at[peer], device_id=(expert, peer * 2 + core), device_id_type=MESH,
        ).wait_recv()

    a_args = (lambda c: train_out.at[c], lambda c: train_in.at[c], a_send, a_recv)
    a_copies = to_peers(*a_args)
    pair_copy = pltpu.make_async_remote_copy(
        src_ref=factor_hbm, dst_ref=factor.at[core], send_sem=pair_send, recv_sem=pair_recv,
        device_id=(expert, mate), device_id_type=MESH,
    )
    pair_copy.start()
    train_in[chip] = train_out[chip]
    own_copy.wait()
    pair_copy.wait_recv()
    for k in range(n_chip - 1):
        from_peer(*a_args, k)

    rows = train_in[...].astype(jnp.float32).reshape(t_plane, wide)
    first = rows[:, :depth].astype(jnp.bfloat16)
    second = rows[:, depth:].astype(jnp.bfloat16)
    share = jnp.dot(first, factor[0], preferred_element_type=jnp.float32)
    share = share + jnp.dot(second, factor[1], preferred_element_type=jnp.float32)
    share = share.reshape(n_chip, t_loc, share.shape[-1])
    part[...] = share
    part_out[...] = share.astype(jnp.bfloat16)
    half_chips = n_chip // 2
    base = chip // half_chips * half_chips
    near = [base + lax.rem(chip - base + k, half_chips) for k in range(1, half_chips)]
    far = [n_chip - half_chips - base + lax.rem(chip - base + k, half_chips) for k in range(half_chips)]
    order = [(peer, part_out, part_in) for peer in far] + [(peer, part, near_in) for peer in near]

    def share_copy(k, slot, peer, source, target):
        return pltpu.make_async_remote_copy(
            src_ref=source.at[peer], dst_ref=target.at[slot], send_sem=b_send.at[k],
            recv_sem=b_recv.at[slot], device_id=(expert, peer * 2 + core), device_id_type=MESH,
        )

    b_copies = [share_copy(k, chip, *entry) for k, entry in enumerate(order)]
    for copy in b_copies:
        copy.start()
    total = part[chip]
    for k, (peer, source, target) in reversed(list(enumerate(order))):
        share_copy(k, peer, peer, source, target).wait_recv()
        total = total + target[peer].astype(jnp.float32)
    at_row = lax.broadcasted_iota(jnp.int32, total.shape, 0)
    weight = jnp.zeros(total.shape, jnp.float32)
    for i in range(t_loc):
        weight = jnp.where(at_row == i, counts_ref[0, i].astype(jnp.float32) / TOKS_EX, weight)
    pre_out[...] = (total * weight).astype(jnp.bfloat16)

    c_args = (lambda c: pre_out, lambda c: pre_in.at[c], c_send, c_recv)
    c_copies = to_peers(*c_args)
    pre_in[chip] = pre_out[...]
    for k in range(n_chip - 1):
        from_peer(*c_args, k)
    pre = pre_in[...].astype(jnp.float32).reshape(t_plane, pre_in.shape[-1]).astype(jnp.bfloat16)
    halves = [
        lax.dot_general(factor[c], pre, NT, preferred_element_type=jnp.float32) for c in range(2)
    ]
    ker[core, chip] = jnp.concatenate(halves, axis=1).astype(jnp.bfloat16)

    d_args = (lambda c: ker.at[core, chip], lambda c: ker.at[core, c], d_send, d_recv)
    d_copies = to_peers(*d_args)
    f_copies = []

    def pass_on(c, k):
        copy = pltpu.make_async_remote_copy(
            src_ref=ker.at[core, c], dst_ref=ker.at[core, c], send_sem=f_send.at[k],
            recv_sem=f_recv.at[c], device_id=(expert, mate), device_id_type=MESH,
        )
        copy.start()
        f_copies.append(copy)

    pass_on(chip, n_chip - 1)
    for k in range(n_chip - 1):
        from_peer(*d_args, k)
        pass_on(peers[k], k)
    for c in range(n_chip):
        pltpu.make_async_remote_copy(
            src_ref=ker.at[1 - core, c], dst_ref=ker.at[1 - core, c], send_sem=f_send.at[c],
            recv_sem=f_recv.at[c], device_id=(expert, mate), device_id_type=MESH,
        ).wait_recv()

    t_all = 2 * t_plane
    for c in range(n_chip):
        even, odd = ker[0, c].astype(jnp.float32), ker[1, c].astype(jnp.float32)
        for half in range(2):
            cols = slice(half * t_plane, (half + 1) * t_plane)
            start = (2 * c + half) * depth
            both = jnp.concatenate([even[:, cols], odd[:, cols]], axis=1)
            kmat[start:start + depth, :] = both.astype(kmat.dtype)

    query_copy.wait()
    matrix = kmat[...].astype(jnp.bfloat16)
    step = query.shape[0] // CHUNKS
    t_out = t_all // n_exp
    e_copies = []
    for i in range(CHUNKS):
        found = jnp.dot(query[i * step:(i + 1) * step, :], matrix, preferred_element_type=jnp.float32).T
        pieces = []
        for c in range(n_chip):
            for plane in range(2):
                start = plane * t_plane + c * t_loc
                pieces.append(found[start:start + t_loc, :])
        ordered = jnp.concatenate(pieces, axis=0)
        for g in range(n_exp):
            block = ordered[g * t_out:(g + 1) * t_out, :]
            score[g, i] = block
            score_out[g, i] = block.astype(jnp.bfloat16)
        for k, rival in enumerate(rivals):
            copy = pltpu.make_async_remote_copy(
                src_ref=score_out.at[rival, i], dst_ref=score_in.at[expert, i],
                send_sem=e_send.at[k, i], recv_sem=e_recv.at[expert, i],
                device_id=(rival, blk), device_id_type=MESH,
            )
            copy.start()
            e_copies.append(copy)
    for i in range(CHUNKS):
        total = score[expert, i]
        for k, rival in enumerate(rivals):
            pltpu.make_async_remote_copy(
                src_ref=score_out.at[rival, i], dst_ref=score_in.at[rival, i],
                send_sem=e_send.at[k, i], recv_sem=e_recv.at[rival, i],
                device_id=(rival, blk), device_id_type=MESH,
            ).wait_recv()
            total = total + score_in[rival, i].astype(jnp.float32)
        out_ref[:, i * step:(i + 1) * step] = total
    pair_copy.wait_send()
    for copy in a_copies + b_copies + c_copies + d_copies + f_copies + e_copies:
        copy.wait_send()


def on_device(n_exp, n_blk, query_grads, train_grads, counts, factor):
    n_chip = n_blk // 2
    query_grads, train_grads, factor = query_grads[0], train_grads[0], factor[0]
    q_loc, width = query_grads.shape
    t_loc, depth = train_grads.shape[0], factor.shape[0]
    t_plane = t_loc * n_chip
    t_all = 2 * t_plane
    t_out = t_all // n_exp
    bf16, f32 = jnp.bfloat16, jnp.float32
    vmem = pl.BlockSpec(memory_space=pltpu.VMEM)
    hbm = pl.BlockSpec(memory_space=pl.ANY)
    dma = pltpu.SemaphoreType.DMA
    transposed = pl.pallas_call(
        functools.partial(kernel, n_exp, n_chip),
        out_shape=jax.ShapeDtypeStruct((t_out, q_loc), f32),
        in_specs=[pl.BlockSpec(memory_space=pltpu.SMEM), vmem, hbm, hbm],
        out_specs=vmem,
        scratch_shapes=[
            pltpu.VMEM((q_loc, width), bf16),
            pltpu.VMEM((2, depth, width), bf16),
            pltpu.VMEM((n_chip, t_loc, 2 * depth), bf16),
            pltpu.VMEM((n_chip, t_loc, 2 * depth), bf16),
            pltpu.VMEM((n_chip, t_loc, width), f32),
            pltpu.VMEM((n_chip, t_loc, width), bf16),
            pltpu.VMEM((n_chip, t_loc, width), bf16),
            pltpu.VMEM((n_chip, t_loc, width), f32),
            pltpu.VMEM((t_loc, width), bf16),
            pltpu.VMEM((n_chip, t_loc, width), bf16),
            pltpu.VMEM((2, n_chip, depth, 2 * t_plane), bf16),
            pltpu.VMEM((width, t_all), bf16 if depth % 16 == 0 else f32),
            pltpu.VMEM((n_exp, CHUNKS, t_out, q_loc // CHUNKS), f32),
            pltpu.VMEM((n_exp, CHUNKS, t_out, q_loc // CHUNKS), bf16),
            pltpu.VMEM((n_exp, CHUNKS, t_out, q_loc // CHUNKS), bf16),
            dma, dma, dma, dma,
            dma((n_chip,)), dma((n_chip,)), dma((n_chip,)), dma((n_chip,)),
            dma((n_chip,)), dma((n_chip,)), dma((n_chip,)), dma((n_chip,)),
            dma((n_chip,)), dma((n_chip,)), dma((n_exp, CHUNKS)), dma((n_exp, CHUNKS)),
        ],
        compiler_params=pltpu.CompilerParams(collective_id=0, has_side_effects=True),
        name="influence",
    )(counts, train_grads, query_grads, factor)
    return transposed.T


def solution(mesh):
    return jax.shard_map(
        functools.partial(on_device, mesh.shape["expert"], mesh.shape["blk"]),
        mesh=mesh,
        in_specs=(
            P("expert", "blk", None),
            P("expert", "blk", None),
            P("expert", "blk"),
            P("expert", "blk", None),
        ),
        out_specs=P("blk", "expert"),
        check_vma=False,
    )
```
